256 devices in a mesh: rows: 16 (over z, core), feat: 16 (over x, y).
Axes of the slice: x: 4, y: 4, z: 8, core: 2. Of those that a mesh axis runs over, the one named last changes fastest.
Arguments:
- features: bfloat16 [16384, 16384], P('rows', 'feat'), may hold values from -0.046875 to 0.046875
- inverse_gram: float32 [16384, 1024], P('feat'), as said below
- targets: float32 [128, 16384], P('feat', 'rows'), may hold values from -6 to 6
Outputs:
- weights: float32 [128, 16384], P(None, 'feat')
- residual: float32 [128, 16384], P('feat', 'rows')
The draws below stay inside these ranges and needn't reach their ends.
Inputs may be any that keep to these rules, and one draw needn't show every extreme that they name: Each block of inverse_gram is symmetric.
All inputs are finite; a program needn't handle non-finite values.
Results may differ from the reference program's by a relative error of at most 0.007.
Values sent between devices are 32-bit elements; how exact they have to be, the bound alone decides.
No kernel may reach another device: no remote copies, remote signals or barrier semaphores. Data moves between devices by JAX's collectives and lax.ppermute only.
A program may use at most 64 MiB of HBM per device.

```python
import math
import jax
import jax.numpy as jnp
from jax import lax

FB = 1024
TGT = 128
TURNS = 2
ROWS = 16384
FEAT = 16384
N_FEAT = 16


ridge_weight = 0.5


def draw_inverse_gram(key, part):
    block_total = FEAT // FB
    first_key, second_key = jax.random.split(key)
    raw_values = jax.random.normal(first_key, (block_total, FB, FB), jnp.float32)
    base_scale = 0.8 / (1.0 + ridge_weight)
    symmetric = (raw_values + jnp.swapaxes(raw_values, 1, 2)) * (0.25 * base_scale / math.sqrt(2.0 * FB))
    diagonal = jax.random.uniform(second_key, (block_total, FB), jnp.float32, 0.8, 1.2) * base_scale
    matrix = symmetric + jnp.eye(FB, dtype=jnp.float32)[None] * diagonal[:, :, None]
    return matrix.reshape(FEAT, FB)


def level_of(key, shape, cuts, low, high):
    factor_of, own = 1.0, jax.random.fold_in(key, 6)
    for dim, shards_of in cuts:
        draws = jnp.exp(jax.random.uniform(jax.random.fold_in(own, dim), (shards_of,), jnp.float32, low / len(cuts), high / len(cuts)))
        factor_of = factor_of * jnp.repeat(draws, shape[dim] // shards_of).reshape([-1 if axis == dim else 1 for axis in range(len(shape))])
    return factor_of


def scatter_about(stream_key, extent, scale, limit, pieces=(), kind=jnp.bfloat16):
    drawn = jax.random.normal(stream_key, extent, jnp.float32) * scale
    if len(pieces) > 0:
        drawn = level_of(stream_key, extent, pieces, -0.22, 0.18) * drawn
    return jnp.clip(drawn, min=-limit, max=limit).astype(kind)


def setup_inputs(seed: int = 0) -> dict:
    streams_of = jax.random.split(jax.random.key(seed), 4)
    features = scatter_about(streams_of[0], (ROWS, FEAT), ROWS ** -0.5, 0.046875, ((0, 16), (1, 16)))
    inverse_gram = draw_inverse_gram(jax.random.fold_in(streams_of[3], 71), 0)
    targets = scatter_about(streams_of[2], (TGT, ROWS), 1.0, 6.0, ((0, 16), (1, 16)), jnp.float32)
    return {"features": features, "inverse_gram": inverse_gram, "targets": targets}


ridge_weight = 0.5


def reference(features, inverse_gram, targets):
    block_count = N_FEAT
    panel_width = TGT // block_count
    feature_blocks = features.astype(jnp.float32).reshape(ROWS, block_count, FB)
    inverse_blocks = inverse_gram.reshape(block_count, FB, FB)
    residual = targets.reshape(block_count, panel_width, ROWS)
    weights = jnp.zeros((block_count, block_count, panel_width, FB), jnp.float32)
    blocks = jnp.arange(block_count, dtype=jnp.int32)
    for section in range(TURNS * block_count):
        panel_index = ((blocks - section) % block_count).astype(jnp.int32)
        rounded = lax.optimization_barrier(residual.astype(jnp.bfloat16)).astype(jnp.float32)
        projection = jnp.einsum("bpr,rbn->bpn", rounded, feature_blocks, precision=lax.Precision.HIGHEST)
        chosen = weights[blocks, panel_index]
        increment = jnp.einsum("bpn,bnm->bpm", projection - ridge_weight * chosen, inverse_blocks, precision=lax.Precision.HIGHEST)
        weights = weights.at[blocks, panel_index].add(increment)
        rounded_increment = lax.optimization_barrier(increment.astype(jnp.bfloat16)).astype(jnp.float32)
        residual = residual - jnp.einsum("bpn,rbn->bpr", rounded_increment, feature_blocks, precision=lax.Precision.HIGHEST)
        residual = jnp.roll(residual, 1, axis=0)
    fitted = jnp.transpose(weights, (1, 2, 0, 3)).reshape(TGT, FEAT)
    return fitted, residual.reshape(TGT, ROWS)
```

```python
import jax
import jax.numpy as jnp
from jax import lax
from jax.sharding import Mesh, PartitionSpec as P

TGT = 128
TURNS = 2
HALF = 2

ridge_weight = 0.5
BF = jnp.bfloat16
F32 = jnp.float32


def passed_along(block, axes, count, distance):
    route = [(i, (i + distance) % count) for i in range(count)]
    return lax.ppermute(block, axes, route)


def dot(a, b, dims=(((1,), (0,)), ((), ()))):
    return lax.dot_general(a, b, dims, preferred_element_type=F32)


def split_dot(a, b):
    high = b.astype(BF)
    low = (b - high.astype(F32)).astype(BF)
    return dot(a, high) + dot(a, low)


def local(features, inverse_gram, targets):
    block_count = lax.axis_size("x") * lax.axis_size("y")
    depth = lax.axis_size("z")
    position = lax.axis_index(("x", "y"))
    core = lax.axis_index("core")
    width = targets.shape[0]
    rows, columns = features.shape
    half = columns // HALF

    one = 1.0 + jnp.minimum(core, 0).astype(F32)

    def other_core(block):
        return passed_along(block, "core", HALF, 1) * one

    def in_order(mine, theirs, dim):
        first = jnp.where(core == 0, mine, theirs)
        second = jnp.where(core == 0, theirs, mine)
        return jnp.concatenate([first, second], dim)

    def half_of(block, which):
        return lax.dynamic_slice_in_dim(block, which * half, half, 1)

    gained = split_dot(features, inverse_gram)
    own_z = half_of(features, core)
    own_h = half_of(gained, core)
    sent_z = half_of(features, 1 - core).astype(F32)
    sent_h = half_of(gained, 1 - core)
    chip_z = in_order(own_z, other_core(sent_z).astype(BF), 0)
    chip_h = in_order(own_h.astype(BF), other_core(sent_h).astype(BF), 0)
    residual = in_order(targets, other_core(targets), 1)

    def section(residual, ridge_term):
        part = dot(residual.astype(BF), chip_h)
        parts = lax.all_to_all(jnp.broadcast_to(part[None], (depth, width, half)), "z", 0, 0)
        increment = jnp.sum(parts, 0)
        if ridge_term is not None:
            increment = increment - ridge_term
        update = dot(increment.astype(BF), chip_z, (((1,), (1,)), ((), ())))
        residual = residual - in_sum(update)
        residual = passed_along(residual, ("x", "y"), block_count, 1)
        return residual, increment

    def in_sum(update):
        return update + passed_along(update, "core", HALF, 1)

    def first_turn(step, carried):
        residual, kept_weights = carried
        residual, increment = section(residual, None)
        return residual, lax.dynamic_update_slice_in_dim(kept_weights, increment[None], step, 0)

    weights = jnp.zeros((block_count, width, half), F32)
    residual, weights = lax.fori_loop(0, block_count, first_turn, (residual, weights))
    flat = weights.reshape(block_count * width, half)
    whole = in_order(flat, passed_along(flat, "core", HALF, 1), 1)
    ridge_terms = ridge_weight * jnp.dot(
        whole, half_of(inverse_gram, core), precision=lax.Precision.HIGHEST
    )
    ridge_terms = ridge_terms.reshape(block_count, width, half)

    def second_turn(step, carried):
        residual, kept_weights = carried
        term = lax.dynamic_index_in_dim(ridge_terms, step, 0, False)
        old = lax.dynamic_index_in_dim(kept_weights, step, 0, False)
        residual, increment = section(residual, term)
        return residual, lax.dynamic_update_slice_in_dim(
            kept_weights, (old + increment)[None], step, 0
        )

    residual, weights = lax.fori_loop(0, block_count, second_turn, (residual, weights))

    order = (position - jnp.arange(block_count)) % block_count
    weights = weights[order].reshape(block_count * width, half)
    weights = in_order(weights, passed_along(weights, "core", HALF, 1), 1)
    return weights, lax.dynamic_slice_in_dim(residual, core * rows, rows, 1)


def solution(mesh):
    inner = Mesh(mesh.devices.reshape(-1, HALF, 4, 4), ("z", "core", "x", "y"))
    rows, feat = ("z", "core"), ("x", "y")
    return jax.shard_map(
        local,
        mesh=inner,
        in_specs=(P(rows, feat), P(feat, None), P(feat, rows)),
        out_specs=(P(None, feat), P(feat, rows)),
        check_vma=False,
    )
```

```python
import jax
import jax.numpy as jnp
from jax import lax
from jax.experimental import pallas as pl
from jax.experimental.pallas import tpu as pltpu
from jax.experimental.layout import Layout, with_layout_constraint
from jax.sharding import Mesh, PartitionSpec as P

TGT = 128
TURNS = 2
HALF = 2

ridge_weight = 0.5
BF = jnp.bfloat16
F32 = jnp.float32


def turned(x):
    return with_layout_constraint(x.T, Layout((0, 1)))


def projected(residual, h, copies, terms=None, at=None, steps=4):
    width, deep = residual.shape
    wide = h.shape[1]
    chunk = deep // steps

    def kernel(at_ref, r_ref, h_ref, *refs):
        term_ref = refs[0] if terms is not None else None
        out_ref, acc_ref = refs[-2:]
        step = pl.program_id(0)

        @pl.when(step == 0)
        def _():
            acc_ref[...] = jnp.zeros_like(acc_ref) if terms is None else -term_ref[0]

        acc_ref[...] += jnp.dot(r_ref[...].astype(BF), h_ref[...], preferred_element_type=F32)

        @pl.when(step == steps - 1)
        def _():
            out_ref[...] = jnp.broadcast_to(acc_ref[...][None], out_ref.shape)

    extra = [] if terms is None else [pl.BlockSpec((1, width, wide), lambda i, at: (at[0], 0, 0))]
    return pl.pallas_call(
        kernel,
        grid_spec=pltpu.PrefetchScalarGridSpec(
            num_scalar_prefetch=1,
            grid=(steps,),
            in_specs=[
                pl.BlockSpec((width, chunk), lambda i, at: (0, i)),
                pl.BlockSpec((chunk, wide), lambda i, at: (i, 0)),
            ] + extra,
            out_specs=pl.BlockSpec((copies, width, wide), lambda i, at: (0, 0, 0)),
            scratch_shapes=[pltpu.VMEM((width, wide), F32)],
        ),
        out_shape=jax.ShapeDtypeStruct((copies, width, wide), F32),
        compiler_params=pltpu.CompilerParams(vmem_limit_bytes=16 << 20),
        cost_estimate=pl.CostEstimate(
            flops=2 * width * deep * wide, bytes_accessed=2 * deep * wide, transcendentals=0
        ),
        name="projected",
    )(at, residual, h, *([] if terms is None else [terms]))


def corrected(parts, zt, steps=4):
    copies, width, wide = parts.shape
    deep = zt.shape[1]
    chunk = deep // steps

    def kernel(parts_ref, z_ref, inc_ref, out_ref, low_ref):
        @pl.when(pl.program_id(0) == 0)
        def _():
            total = parts_ref[0]
            for i in range(1, copies):
                total = total + parts_ref[i]
            inc_ref[...] = total
            low_ref[...] = total.astype(BF)

        out_ref[...] = jnp.dot(low_ref[...], z_ref[...], preferred_element_type=F32)

    whole = pl.BlockSpec((width, wide), lambda i: (0, 0))
    return pl.pallas_call(
        kernel,
        grid=(steps,),
        in_specs=[
            pl.BlockSpec((copies, width, wide), lambda i: (0, 0, 0)),
            pl.BlockSpec((wide, chunk), lambda i: (0, i)),
        ],
        out_specs=[whole, pl.BlockSpec((width, chunk), lambda i: (0, i))],
        out_shape=[
            jax.ShapeDtypeStruct((width, wide), F32),
            jax.ShapeDtypeStruct((width, deep), F32),
        ],
        scratch_shapes=[pltpu.VMEM((width, wide), BF)],
        compiler_params=pltpu.CompilerParams(vmem_limit_bytes=16 << 20),
        cost_estimate=pl.CostEstimate(
            flops=2 * width * deep * wide, bytes_accessed=2 * deep * wide, transcendentals=0
        ),
        name="corrected",
    )(parts, zt)


def passed_along(block, axes, count, distance):
    route = [(i, (i + distance) % count) for i in range(count)]
    return lax.ppermute(block, axes, route)


def dot(a, b, dims=(((1,), (0,)), ((), ()))):
    return lax.dot_general(a, b, dims, preferred_element_type=F32)


def split_dot(a, b):
    high = b.astype(BF)
    low = (b - high.astype(F32)).astype(BF)
    return dot(a, high) + dot(a, low)


def local(features, inverse_gram, targets):
    block_count = lax.axis_size("x") * lax.axis_size("y")
    depth = lax.axis_size("z")
    position = lax.axis_index(("x", "y"))
    core = lax.axis_index("core")
    width = targets.shape[0]
    rows, columns = features.shape
    half = columns // HALF

    one = 1.0 + jnp.minimum(core, 0).astype(F32)

    def other_core(block):
        return passed_along(block, "core", HALF, 1) * one

    def in_order(mine, theirs, dim):
        first = jnp.where(core == 0, mine, theirs)
        second = jnp.where(core == 0, theirs, mine)
        return jnp.concatenate([first, second], dim)

    def half_of(block, which):
        return lax.dynamic_slice_in_dim(block, which * half, half, 1)

    def swapped(block):
        return passed_along(block, "core", HALF, 1)

    residual = in_order(targets, swapped(targets), 1)
    theirs = other_core(features.astype(F32)).astype(BF)
    my_gram = half_of(inverse_gram, core)
    chip_h = in_order(split_dot(features, my_gram), split_dot(theirs, my_gram), 0).astype(BF)
    chip_z = turned(half_of(in_order(features, theirs, 0), core))

    def section(residual, at, terms=None):
        parts = lax.all_to_all(projected(residual, chip_h, depth, terms, at), "z", 0, 0)
        increment, update = corrected(parts, chip_z)
        residual = residual - (update + swapped(update))
        return passed_along(residual, ("x", "y"), block_count, 1), increment

    def turn(residual, made, terms):
        def one_section(step, carried):
            residual, made, at = carried
            residual, increment = section(residual, at, terms)
            return residual, lax.dynamic_update_slice_in_dim(made, increment[None], step, 0), at + 1

        at = jnp.zeros((1,), jnp.int32)
        return lax.fori_loop(0, block_count, one_section, (residual, made, at))[:2]

    residual, weights = turn(residual, jnp.zeros((block_count, width, half), F32), None)
    flat = weights.reshape(block_count * width, half)
    whole = in_order(flat, swapped(flat), 1)
    terms = ridge_weight * jnp.dot(whole, my_gram, precision=lax.Precision.HIGHEST)
    terms = jnp.where(lax.axis_index("z") == 0, terms, 0.0).reshape(block_count, width, half)
    residual, more = turn(residual, jnp.zeros_like(weights), terms)
    weights = weights + more

    order = (position - jnp.arange(block_count)) % block_count
    weights = weights[order].reshape(block_count * width, half)
    weights = in_order(weights, passed_along(weights, "core", HALF, 1), 1)
    return weights, lax.dynamic_slice_in_dim(residual, core * rows, rows, 1)


def solution(mesh):
    inner = Mesh(mesh.devices.reshape(-1, HALF, 4, 4), ("z", "core", "x", "y"))
    rows, feat = ("z", "core"), ("x", "y")
    return jax.shard_map(
        local,
        mesh=inner,
        in_specs=(P(rows, feat), P(feat, None), P(feat, rows)),
        out_specs=(P(None, feat), P(feat, rows)),
        check_vma=False,
    )
```

```python
import jax
import jax.numpy as jnp
from jax import lax
from jax.experimental import pallas as pl
from jax.experimental.pallas import tpu as pltpu
from jax.experimental.layout import Layout, with_layout_constraint
from jax.sharding import Mesh, PartitionSpec as P

TGT = 128
TURNS = 2
HALF = 2

ridge_weight = 0.5
BF = jnp.bfloat16
F32 = jnp.float32


def turned(x):
    return with_layout_constraint(x.T, Layout((0, 1)))


def projected(residual, hs, copies, at, terms=None, steps=4):
    width, deep = residual.shape
    widths = [h.shape[1] for h in hs]
    wide = sum(widths)
    chunk = deep // steps
    count = len(hs)

    def kernel(at_ref, r_ref, *refs):
        h_refs, refs = refs[:count], refs[count:]
        held_refs, sem_ref = refs[-count - 1 : -1], refs[-1]
        out_ref = refs[-count - 2]
        started = []
        for step in range(steps):
            for i, (h_ref, held_ref) in enumerate(zip(h_refs, held_refs)):
                place = pl.ds(step * chunk, chunk)
                copy = pltpu.make_async_copy(
                    h_ref.at[place], held_ref.at[place], sem_ref.at[i, step]
                )
                copy.start()
                started.append((i, step, copy))
        sums = [None] * count
        for i, step, copy in started:
            low = r_ref[:, step * chunk : (step + 1) * chunk].astype(BF)
            copy.wait()
            held = held_refs[i][step * chunk : (step + 1) * chunk]
            more = jnp.dot(low, held, preferred_element_type=F32)
            sums[i] = more if sums[i] is None else sums[i] + more
        for i, total in enumerate(sums):
            place = slice(sum(widths[:i]), sum(widths[: i + 1]))
            if terms is not None:
                total = total - refs[0][0, :, place]
            out_ref[:, :, place] = jnp.broadcast_to(total[None], (copies, *total.shape))

    extra = [] if terms is None else [pl.BlockSpec((1, width, wide), lambda i, at: (at[0], 0, 0))]
    return pl.pallas_call(
        kernel,
        grid_spec=pltpu.PrefetchScalarGridSpec(
            num_scalar_prefetch=1,
            grid=(1,),
            in_specs=[pl.BlockSpec((width, deep), lambda i, at: (0, 0))]
            + [pl.BlockSpec(memory_space=pl.ANY) for _ in hs]
            + extra,
            out_specs=pl.BlockSpec((copies, width, wide), lambda i, at: (0, 0, 0)),
            scratch_shapes=[pltpu.VMEM((deep, each), BF) for each in widths]
            + [pltpu.SemaphoreType.DMA((count, steps))],
        ),
        out_shape=jax.ShapeDtypeStruct((copies, width, wide), F32),
        compiler_params=pltpu.CompilerParams(vmem_limit_bytes=16 << 20),
        cost_estimate=pl.CostEstimate(
            flops=2 * width * deep * wide, bytes_accessed=2 * deep * wide, transcendentals=0
        ),
        name="projected",
    )(at, residual, *hs, *([] if terms is None else [terms]))


def corrected(parts, zts, steps=4):
    copies, width, wide = parts.shape
    heights = [zt.shape[0] for zt in zts]
    deep = zts[0].shape[1]
    chunk = deep // steps
    count = len(zts)

    def kernel(parts_ref, *refs):
        z_refs = refs[:count]
        inc_ref, out_ref, low_ref = refs[count:]

        @pl.when(pl.program_id(0) == 0)
        def _():
            total = parts_ref[0]
            for i in range(1, copies):
                total = total + parts_ref[i]
            inc_ref[...] = total
            low_ref[...] = total.astype(BF)

        update = None
        for i, z_ref in enumerate(z_refs):
            place = slice(sum(heights[:i]), sum(heights[: i + 1]))
            more = jnp.dot(low_ref[:, place], z_ref[...], preferred_element_type=F32)
            update = more if update is None else update + more
        out_ref[...] = update

    whole = pl.BlockSpec((width, wide), lambda i: (0, 0))
    return pl.pallas_call(
        kernel,
        grid=(steps,),
        in_specs=[pl.BlockSpec((copies, width, wide), lambda i: (0, 0, 0))]
        + [pl.BlockSpec((each, chunk), lambda i: (0, i)) for each in heights],
        out_specs=[whole, pl.BlockSpec((width, chunk), lambda i: (0, i))],
        out_shape=[
            jax.ShapeDtypeStruct((width, wide), F32),
            jax.ShapeDtypeStruct((width, deep), F32),
        ],
        scratch_shapes=[pltpu.VMEM((width, wide), BF)],
        compiler_params=pltpu.CompilerParams(vmem_limit_bytes=16 << 20),
        cost_estimate=pl.CostEstimate(
            flops=2 * width * deep * wide, bytes_accessed=2 * deep * wide, transcendentals=0
        ),
        name="corrected",
    )(parts, *zts)


def dot(a, b, dims=(((1,), (0,)), ((), ()))):
    return lax.dot_general(a, b, dims, preferred_element_type=F32)


def split_dot(a, b):
    high = b.astype(BF)
    low = (b - high.astype(F32)).astype(BF)
    return dot(a, high) + dot(a, low)


def exact_dot(a, b):
    return jnp.dot(a, b, precision=lax.Precision.HIGHEST)


def after(x, *others):
    return lax.optimization_barrier((x, *others))[0]


def local(features, inverse_gram, targets):
    blocks = lax.axis_size("x") * lax.axis_size("y")
    depth = lax.axis_size("z")
    position = lax.axis_index(("x", "y"))
    core = lax.axis_index("core")
    z = lax.axis_index("z")
    width = targets.shape[0]
    rows, columns = features.shape
    half = columns // HALF
    pairs = blocks // 2
    one = 1.0 + jnp.minimum(core, 0).astype(F32)

    def swapped(block):
        return lax.ppermute(block, "core", [(0, 1), (1, 0)])

    def moved(block, distance):
        route = [(i, (i + distance) % blocks) for i in range(blocks)]
        return lax.ppermute(block, ("x", "y"), route)

    def in_order(mine, theirs, dim):
        first = jnp.where(core == 0, mine, theirs)
        second = jnp.where(core == 0, theirs, mine)
        return jnp.concatenate([first, second], dim)

    def half_of(block, which, dim=1):
        return lax.dynamic_slice_in_dim(block, which * half, half, dim)

    def from_other(block):
        return (swapped(block.astype(F32)) * one).astype(BF)

    my_gram = half_of(inverse_gram, core)
    share = columns // depth
    gram_piece = moved(lax.dynamic_slice_in_dim(my_gram, z * share, share, 0), 1)
    residual = moved(in_order(targets, swapped(targets), 1), 1)
    before_own = moved(after(features.astype(F32), gram_piece, residual), 1)
    before_gram = lax.all_gather(gram_piece, "z", axis=0, tiled=True)

    theirs = from_other(features)
    full = in_order(features, theirs, 0)
    h = in_order(split_dot(features, my_gram), split_dot(theirs, my_gram), 0)
    zt = turned(half_of(full, core))
    low_h = h.astype(BF)

    before_own = after(before_own, h, low_h, zt, full, before_gram)
    before_near = half_of(before_own, core)
    before_far = half_of(before_own, 1 - core)
    got = swapped(before_far)
    before = in_order((before_near * one).astype(BF), (got * one).astype(BF), 0)
    part = dot(before, full, (((0,), (0,)), ((), ())))
    cross = lax.psum_scatter(part, "z", scatter_dimension=0, tiled=True)
    got = swapped(after(before_near, part))
    other = in_order((before_far * one).astype(BF), (got * one).astype(BF), 0)
    before_full = jnp.concatenate(
        [jnp.where(core == 0, before, other), jnp.where(core == 0, other, before)], 1
    )
    before_h = split_dot(before_full, before_gram).astype(BF)
    before_zt = turned(before)

    def settled(residual, update):
        return residual - (update + swapped(update))

    def solved(residual, hs, zts, at, terms=None):
        parts = lax.all_to_all(projected(residual, hs, depth, at, terms), "z", 0, 0)
        return corrected(parts, zts)

    def one_by_one(residual):
        at = jnp.zeros((1,), jnp.int32)
        first, update = solved(residual, [before_h], [before_zt], at)
        residual = settled(residual, update)
        second, update = solved(residual, [low_h], [zt], at)
        return residual, update, jnp.concatenate([first, second], 1)

    residual, update, made_0 = one_by_one(residual)
    cross = after(cross, update)
    through = lax.all_gather(exact_dot(cross, inverse_gram), "z", axis=0, tiled=True)
    residual = moved(settled(residual, update), 2)
    residual, update, made_1 = one_by_one(residual)
    residual = settled(residual, update)
    through = after(through, residual)
    residual = moved(residual, 2)

    product = split_dot(before_h, through)
    product = half_of(product, core) + swapped(half_of(product, 1 - core))
    hs, zts = [before_h, (h - product).astype(BF)], [before_zt, zt]

    def rounds(residual, made, first, terms):
        def one_round(step, carried):
            residual, made, at = carried
            increment, update = solved(residual, hs, zts, at, terms)
            residual = moved(settled(residual, update), 2)
            made = lax.dynamic_update_slice_in_dim(made, increment[None], step, 0)
            return residual, made, at + 1

        at = jnp.full((1,), first, jnp.int32)
        return lax.fori_loop(first, pairs, one_round, (residual, made, at))[:2]

    made = jnp.zeros((pairs, width, columns), F32)
    made = lax.dynamic_update_slice_in_dim(made, jnp.stack([made_0, made_1]), 0, 0)
    residual, made = rounds(residual, made, 2, None)

    flat = made.reshape(pairs * width, columns)
    got = swapped(flat)
    before_whole = in_order(flat[:, :half], got[:, :half], 1)
    here_whole = in_order(flat[:, half:], got[:, half:], 1)
    before_term = ridge_weight * exact_dot(before_whole, before_gram)
    here_term = ridge_weight * exact_dot(here_whole, my_gram)
    carried = exact_dot(before_term, through)
    carried = half_of(carried, core) + swapped(half_of(carried, 1 - core))
    terms = jnp.concatenate([before_term, here_term - carried], 1)
    terms = jnp.where(z == 0, terms, 0.0).reshape(pairs, width, columns)
    residual, more = rounds(residual, jnp.zeros_like(made), 0, terms)

    residual = moved(lax.dynamic_slice_in_dim(residual, core * rows, rows, 1), -1)
    made = made + more
    weights = jnp.stack([moved(made[:, :, :half], -1), made[:, :, half:]], 1)
    order = (position - jnp.arange(blocks)) % blocks
    weights = weights.reshape(blocks, width, half)[order].reshape(blocks * width, half)
    return in_order(weights, swapped(weights), 1), residual


def solution(mesh):
    inner = Mesh(mesh.devices.reshape(-1, HALF, 4, 4), ("z", "core", "x", "y"))
    rows, feat = ("z", "core"), ("x", "y")
    return jax.shard_map(
        local,
        mesh=inner,
        in_specs=(P(rows, feat), P(feat, None), P(feat, rows)),
        out_specs=(P(None, feat), P(feat, rows)),
        check_vma=False,
    )
```

```python
import jax
import jax.numpy as jnp
from jax import lax
from jax.experimental import pallas as pl
from jax.experimental.pallas import tpu as pltpu
from jax.experimental.layout import Layout, with_layout_constraint
from jax.sharding import Mesh, PartitionSpec as P

TGT = 128
TURNS = 2
HALF = 2

ridge_weight = 0.5
BF = jnp.bfloat16
F32 = jnp.float32


def turned(x):
    return with_layout_constraint(x.T, Layout((0, 1)))


def projected(residual, hs, copies, at, terms=None, steps=4):
    width, deep = residual.shape
    widths = [h.shape[1] for h in hs]
    wide = sum(widths)
    chunk = deep // steps
    count = len(hs)

    def kernel(at_ref, r_ref, *refs):
        h_refs, refs = refs[:count], refs[count:]
        held_refs, sem_ref = refs[-count - 1 : -1], refs[-1]
        out_ref = refs[-count - 2]
        started = []
        for step in range(steps):
            for i, (h_ref, held_ref) in enumerate(zip(h_refs, held_refs)):
                place = pl.ds(step * chunk, chunk)
                copy = pltpu.make_async_copy(
                    h_ref.at[place], held_ref.at[place], sem_ref.at[i, step]
                )
                copy.start()
                started.append((i, step, copy))
        sums = [None] * count
        for i, step, copy in started:
            low = r_ref[:, step * chunk : (step + 1) * chunk].astype(BF)
            copy.wait()
            held = held_refs[i][step * chunk : (step + 1) * chunk]
            more = jnp.dot(low, held, preferred_element_type=F32)
            sums[i] = more if sums[i] is None else sums[i] + more
        for i, total in enumerate(sums):
            place = slice(sum(widths[:i]), sum(widths[: i + 1]))
            if terms is not None:
                total = total - refs[0][0, :, place]
            out_ref[:, :, place] = jnp.broadcast_to(total[None], (copies, *total.shape))

    extra = [] if terms is None else [pl.BlockSpec((1, width, wide), lambda i, at: (at[0], 0, 0))]
    return pl.pallas_call(
        kernel,
        grid_spec=pltpu.PrefetchScalarGridSpec(
            num_scalar_prefetch=1,
            grid=(1,),
            in_specs=[pl.BlockSpec((width, deep), lambda i, at: (0, 0))]
            + [pl.BlockSpec(memory_space=pl.ANY) for _ in hs]
            + extra,
            out_specs=pl.BlockSpec((copies, width, wide), lambda i, at: (0, 0, 0)),
            scratch_shapes=[pltpu.VMEM((deep, each), BF) for each in widths]
            + [pltpu.SemaphoreType.DMA((count, steps))],
        ),
        out_shape=jax.ShapeDtypeStruct((copies, width, wide), F32),
        compiler_params=pltpu.CompilerParams(vmem_limit_bytes=16 << 20),
        cost_estimate=pl.CostEstimate(
            flops=2 * width * deep * wide, bytes_accessed=2 * deep * wide, transcendentals=0
        ),
        name="projected",
    )(at, residual, *hs, *([] if terms is None else [terms]))


def corrected(parts, zts, steps=4):
    copies, width, wide = parts.shape
    heights = [zt.shape[0] for zt in zts]
    deep = zts[0].shape[1]
    chunk = deep // steps
    count = len(zts)

    def kernel(parts_ref, *refs):
        z_refs = refs[:count]
        inc_ref, out_ref, low_ref = refs[count:]

        @pl.when(pl.program_id(0) == 0)
        def _():
            total = parts_ref[0]
            for i in range(1, copies):
                total = total + parts_ref[i]
            inc_ref[...] = total
            low_ref[...] = total.astype(BF)

        update = None
        for i, z_ref in enumerate(z_refs):
            place = slice(sum(heights[:i]), sum(heights[: i + 1]))
            more = jnp.dot(low_ref[:, place], z_ref[...], preferred_element_type=F32)
            update = more if update is None else update + more
        out_ref[...] = update

    whole = pl.BlockSpec((width, wide), lambda i: (0, 0))
    return pl.pallas_call(
        kernel,
        grid=(steps,),
        in_specs=[pl.BlockSpec((copies, width, wide), lambda i: (0, 0, 0))]
        + [pl.BlockSpec((each, chunk), lambda i: (0, i)) for each in heights],
        out_specs=[whole, pl.BlockSpec((width, chunk), lambda i: (0, i))],
        out_shape=[
            jax.ShapeDtypeStruct((width, wide), F32),
            jax.ShapeDtypeStruct((width, deep), F32),
        ],
        scratch_shapes=[pltpu.VMEM((width, wide), BF)],
        compiler_params=pltpu.CompilerParams(vmem_limit_bytes=16 << 20),
        cost_estimate=pl.CostEstimate(
            flops=2 * width * deep * wide, bytes_accessed=2 * deep * wide, transcendentals=0
        ),
        name="corrected",
    )(parts, *zts)


def dot(a, b, dims=(((1,), (0,)), ((), ()))):
    return lax.dot_general(a, b, dims, preferred_element_type=F32)


def split_dot(a, b):
    high = b.astype(BF)
    low = (b - high.astype(F32)).astype(BF)
    return dot(a, high) + dot(a, low)


def exact_dot(a, b):
    return jnp.dot(a, b, precision=lax.Precision.HIGH)


def after(x, *others):
    return lax.optimization_barrier((x, *others))[0]


def local(features, inverse_gram, targets):
    blocks = lax.axis_size("x") * lax.axis_size("y")
    depth = lax.axis_size("z")
    position = lax.axis_index(("x", "y"))
    core = lax.axis_index("core")
    z = lax.axis_index("z")
    width = targets.shape[0]
    rows, columns = features.shape
    half = columns // HALF
    pairs = blocks // 2
    one = 1.0 + jnp.minimum(core, 0).astype(F32)

    def swapped(block):
        return lax.ppermute(block, "core", [(0, 1), (1, 0)])

    def moved(block, distance):
        route = [(i, (i + distance) % blocks) for i in range(blocks)]
        return lax.ppermute(block, ("x", "y"), route)

    def in_order(mine, theirs, dim):
        first = jnp.where(core == 0, mine, theirs)
        second = jnp.where(core == 0, theirs, mine)
        return jnp.concatenate([first, second], dim)

    def half_of(block, which, dim=1):
        return lax.dynamic_slice_in_dim(block, which * half, half, dim)

    def from_other(block):
        return (swapped(block.astype(F32)) * one).astype(BF)

    my_gram = half_of(inverse_gram, core)
    share = columns // depth
    gram_piece = moved(lax.dynamic_slice_in_dim(my_gram, z * share, share, 0), 1)
    residual = moved(in_order(targets, swapped(targets), 1), 1)
    before_own = moved(after(features.astype(F32), gram_piece), 1)
    before_gram = lax.all_gather(gram_piece, "z", axis=0, tiled=True)

    theirs = from_other(features)
    full = in_order(features, theirs, 0)
    h = in_order(split_dot(features, my_gram), split_dot(theirs, my_gram), 0)
    zt = turned(half_of(full, core))
    low_h = h.astype(BF)

    before_own = after(before_own, h, low_h, zt, full, before_gram)
    before_near = half_of(before_own, core)
    before_far = half_of(before_own, 1 - core)
    got = swapped(before_far)
    before = in_order((before_near * one).astype(BF), (got * one).astype(BF), 0)
    part = dot(before, full, (((0,), (0,)), ((), ())))
    cross = lax.psum_scatter(part, "z", scatter_dimension=0, tiled=True)
    got = swapped(after(before_near, part))
    other = in_order((before_far * one).astype(BF), (got * one).astype(BF), 0)
    before_full = jnp.concatenate(
        [jnp.where(core == 0, before, other), jnp.where(core == 0, other, before)], 1
    )
    before_h = split_dot(before_full, before_gram).astype(BF)
    before_zt = turned(before)

    def settled(residual, update):
        return residual - (update + swapped(update))

    def solved(residual, hs, zts, at, terms=None):
        parts = lax.all_to_all(projected(residual, hs, depth, at, terms), "z", 0, 0)
        return corrected(parts, zts)

    def one_by_one(residual):
        at = jnp.zeros((1,), jnp.int32)
        first, update = solved(residual, [before_h], [before_zt], at)
        residual = settled(residual, update)
        second, update = solved(residual, [low_h], [zt], at)
        return residual, update, jnp.concatenate([first, second], 1)

    residual, update, made_0 = one_by_one(residual)
    cross = after(cross, update)
    through = lax.all_gather(exact_dot(cross, inverse_gram), "z", axis=0, tiled=True)
    residual = moved(settled(residual, update), 2)
    residual, update, made_1 = one_by_one(residual)
    residual = settled(residual, update)
    through = after(through, residual)
    residual = moved(residual, 2)

    product = split_dot(before_h, half_of(through, 1 - core))
    product = split_dot(before_h, half_of(through, core)) + swapped(product)
    hs, zts = [before_h, (h - product).astype(BF)], [before_zt, zt]

    def rounds(residual, made, first, terms):
        def one_round(step, carried):
            residual, made, at = carried
            increment, update = solved(residual, hs, zts, at, terms)
            residual = moved(settled(residual, update), 2)
            made = lax.dynamic_update_slice_in_dim(made, increment[None], step, 0)
            return residual, made, at + 1

        at = jnp.full((1,), first, jnp.int32)
        return lax.fori_loop(first, pairs, one_round, (residual, made, at))[:2]

    made = jnp.zeros((pairs, width, columns), F32)
    made = lax.dynamic_update_slice_in_dim(made, jnp.stack([made_0, made_1]), 0, 0)
    residual, made = rounds(residual, made, 2, None)

    flat = made.reshape(pairs * width, columns)
    got = swapped(flat)
    before_whole = in_order(flat[:, :half], got[:, :half], 1)
    here_whole = in_order(flat[:, half:], got[:, half:], 1)
    before_term = ridge_weight * exact_dot(before_whole, before_gram)
    here_term = ridge_weight * exact_dot(here_whole, my_gram)
    carried = exact_dot(before_term, through)
    carried = half_of(carried, core) + swapped(half_of(carried, 1 - core))
    terms = jnp.concatenate([before_term, here_term - carried], 1)
    terms = jnp.where(z == 0, terms, 0.0).reshape(pairs, width, columns)
    residual, more = rounds(residual, jnp.zeros_like(made), 0, terms)

    residual = moved(lax.dynamic_slice_in_dim(residual, core * rows, rows, 1), -1)
    made = made + more
    weights = jnp.stack([moved(made[:, :, :half], -1), made[:, :, half:]], 1)
    order = (position - jnp.arange(blocks)) % blocks
    weights = weights.reshape(blocks, width, half)[order].reshape(blocks * width, half)
    return in_order(weights, swapped(weights), 1), residual


def solution(mesh):
    inner = Mesh(mesh.devices.reshape(-1, HALF, 4, 4), ("z", "core", "x", "y"))
    rows, feat = ("z", "core"), ("x", "y")
    return jax.shard_map(
        local,
        mesh=inner,
        in_specs=(P(rows, feat), P(feat, None), P(feat, rows)),
        out_specs=(P(None, feat), P(feat, rows)),
        check_vma=False,
    )
```

```python
import jax
import jax.numpy as jnp
from jax import lax
from jax.experimental import pallas as pl
from jax.experimental.pallas import tpu as pltpu
from jax.experimental.layout import Layout, with_layout_constraint
from jax.sharding import Mesh, PartitionSpec as P

TGT = 128
TURNS = 2
HALF = 2

ridge_weight = 0.5
BF = jnp.bfloat16
F32 = jnp.float32


def turned(x):
    return with_layout_constraint(x.T, Layout((0, 1)))


def projected(residual, hs, copies, at, terms=None, steps=4):
    width, deep = residual.shape
    widths = [h.shape[1] for h in hs]
    wide = sum(widths)
    chunk = deep // steps
    count = len(hs)

    def kernel(at_ref, r_ref, *refs):
        h_refs, refs = refs[:count], refs[count:]
        held_refs, sem_ref = refs[-count - 1 : -1], refs[-1]
        out_ref = refs[-count - 2]
        started = []
        for step in range(steps):
            for i, (h_ref, held_ref) in enumerate(zip(h_refs, held_refs)):
                place = pl.ds(step * chunk, chunk)
                copy = pltpu.make_async_copy(
                    h_ref.at[place], held_ref.at[place], sem_ref.at[i, step]
                )
                copy.start()
                started.append((i, step, copy))
        sums = [None] * count
        for i, step, copy in started:
            low = r_ref[:, step * chunk : (step + 1) * chunk].astype(BF)
            copy.wait()
            held = held_refs[i][step * chunk : (step + 1) * chunk]
            more = jnp.dot(low, held, preferred_element_type=F32)
            sums[i] = more if sums[i] is None else sums[i] + more
        for i, total in enumerate(sums):
            place = slice(sum(widths[:i]), sum(widths[: i + 1]))
            if terms is not None:
                total = total - refs[0][0, :, place]
            out_ref[:, :, place] = jnp.broadcast_to(total[None], (copies, *total.shape))

    extra = [] if terms is None else [pl.BlockSpec((1, width, wide), lambda i, at: (at[0], 0, 0))]
    return pl.pallas_call(
        kernel,
        grid_spec=pltpu.PrefetchScalarGridSpec(
            num_scalar_prefetch=1,
            grid=(1,),
            in_specs=[pl.BlockSpec((width, deep), lambda i, at: (0, 0))]
            + [pl.BlockSpec(memory_space=pl.ANY) for _ in hs]
            + extra,
            out_specs=pl.BlockSpec((copies, width, wide), lambda i, at: (0, 0, 0)),
            scratch_shapes=[pltpu.VMEM((deep, each), BF) for each in widths]
            + [pltpu.SemaphoreType.DMA((count, steps))],
        ),
        out_shape=jax.ShapeDtypeStruct((copies, width, wide), F32),
        compiler_params=pltpu.CompilerParams(vmem_limit_bytes=16 << 20),
        cost_estimate=pl.CostEstimate(
            flops=2 * width * deep * wide, bytes_accessed=2 * deep * wide, transcendentals=0
        ),
        name="projected",
    )(at, residual, *hs, *([] if terms is None else [terms]))


def corrected(parts, zts, steps=4):
    copies, width, wide = parts.shape
    heights = [zt.shape[0] for zt in zts]
    deep = zts[0].shape[1]
    chunk = deep // steps
    count = len(zts)

    def kernel(parts_ref, *refs):
        z_refs = refs[:count]
        inc_ref, out_ref, low_ref = refs[count:]

        @pl.when(pl.program_id(0) == 0)
        def _():
            total = parts_ref[0]
            for i in range(1, copies):
                total = total + parts_ref[i]
            inc_ref[...] = total
            low_ref[...] = total.astype(BF)

        update = None
        for i, z_ref in enumerate(z_refs):
            place = slice(sum(heights[:i]), sum(heights[: i + 1]))
            more = jnp.dot(low_ref[:, place], z_ref[...], preferred_element_type=F32)
            update = more if update is None else update + more
        out_ref[...] = update

    whole = pl.BlockSpec((width, wide), lambda i: (0, 0))
    return pl.pallas_call(
        kernel,
        grid=(steps,),
        in_specs=[pl.BlockSpec((copies, width, wide), lambda i: (0, 0, 0))]
        + [pl.BlockSpec((each, chunk), lambda i: (0, i)) for each in heights],
        out_specs=[whole, pl.BlockSpec((width, chunk), lambda i: (0, i))],
        out_shape=[
            jax.ShapeDtypeStruct((width, wide), F32),
            jax.ShapeDtypeStruct((width, deep), F32),
        ],
        scratch_shapes=[pltpu.VMEM((width, wide), BF)],
        compiler_params=pltpu.CompilerParams(vmem_limit_bytes=16 << 20),
        cost_estimate=pl.CostEstimate(
            flops=2 * width * deep * wide, bytes_accessed=2 * deep * wide, transcendentals=0
        ),
        name="corrected",
    )(parts, *zts)


def dot(a, b, dims=(((1,), (0,)), ((), ()))):
    return lax.dot_general(a, b, dims, preferred_element_type=F32)


def split_dot(a, b):
    high = b.astype(BF)
    low = (b - high.astype(F32)).astype(BF)
    return dot(a, high) + dot(a, low)


def exact_dot(a, b):
    return jnp.dot(a, b, precision=lax.Precision.HIGH)


def after(x, *others):
    return lax.optimization_barrier((x, *others))[0]


def local(features, inverse_gram, targets):
    blocks = lax.axis_size("x") * lax.axis_size("y")
    depth = lax.axis_size("z")
    position = lax.axis_index(("x", "y"))
    core = lax.axis_index("core")
    z = lax.axis_index("z")
    width = targets.shape[0]
    rows, columns = features.shape
    half = columns // HALF
    pairs = blocks // 2
    one = 1.0 + jnp.minimum(core, 0).astype(F32)

    def swapped(block):
        return lax.ppermute(block, "core", [(0, 1), (1, 0)])

    def moved(block, distance):
        route = [(i, (i + distance) % blocks) for i in range(blocks)]
        return lax.ppermute(block, ("x", "y"), route)

    def in_order(mine, theirs, dim):
        first = jnp.where(core == 0, mine, theirs)
        second = jnp.where(core == 0, theirs, mine)
        return jnp.concatenate([first, second], dim)

    def half_of(block, which, dim=1):
        return lax.dynamic_slice_in_dim(block, which * half, half, dim)

    def from_other(block):
        return (swapped(block.astype(F32)) * one).astype(BF)

    my_gram = half_of(inverse_gram, core)
    share = columns // depth
    gram_piece = moved(lax.dynamic_slice_in_dim(my_gram, z * share, share, 0), 1)
    residual = moved(in_order(targets, swapped(targets), 1), 1)
    large = after(features.astype(F32), gram_piece)
    before_own = moved(large, 1)
    before_gram = lax.all_gather(gram_piece, "z", axis=0, tiled=True)

    theirs = (swapped(large) * one).astype(BF)
    full = in_order(features, theirs, 0)
    h = in_order(split_dot(features, my_gram), split_dot(theirs, my_gram), 0)
    zt = turned(half_of(full, core))
    low_h = h.astype(BF)

    before_own = after(before_own, h, low_h, zt, full, before_gram)
    before_near = half_of(before_own, core)
    before_far = half_of(before_own, 1 - core)
    got = swapped(before_far)
    before = in_order((before_near * one).astype(BF), (got * one).astype(BF), 0)
    part = dot(before, full, (((0,), (0,)), ((), ())))
    cross = lax.psum_scatter(part, "z", scatter_dimension=0, tiled=True)
    got = swapped(after(before_near, part))
    other = in_order((before_far * one).astype(BF), (got * one).astype(BF), 0)
    before_full = jnp.concatenate(
        [jnp.where(core == 0, before, other), jnp.where(core == 0, other, before)], 1
    )
    before_h = split_dot(before_full, before_gram).astype(BF)
    before_zt = turned(before)

    def settled(residual, update):
        return residual - (update + swapped(update))

    def solved(residual, hs, zts, at, terms=None):
        parts = lax.all_to_all(projected(residual, hs, depth, at, terms), "z", 0, 0)
        return corrected(parts, zts)

    def one_by_one(residual):
        at = jnp.zeros((1,), jnp.int32)
        first, update = solved(residual, [before_h], [before_zt], at)
        residual = settled(residual, update)
        second, update = solved(residual, [low_h], [zt], at)
        return residual, update, jnp.concatenate([first, second], 1)

    residual, update, made_0 = one_by_one(residual)
    cross = after(cross, update)
    through = lax.all_gather(exact_dot(cross, inverse_gram), "z", axis=0, tiled=True)
    residual = moved(settled(residual, update), 2)
    residual, update, made_1 = one_by_one(residual)
    residual = settled(residual, update)
    through = after(through, residual)
    residual = moved(residual, 2)

    product = split_dot(before_h, half_of(through, 1 - core))
    product = split_dot(before_h, half_of(through, core)) + swapped(product)
    hs, zts = [before_h, (h - product).astype(BF)], [before_zt, zt]

    def rounds(residual, made, first, terms):
        def one_round(step, carried):
            residual, made, at = carried
            increment, update = solved(residual, hs, zts, at, terms)
            residual = moved(settled(residual, update), 2)
            made = lax.dynamic_update_slice_in_dim(made, increment[None], step, 0)
            return residual, made, at + 1

        at = jnp.full((1,), first, jnp.int32)
        return lax.fori_loop(first, pairs, one_round, (residual, made, at))[:2]

    made = jnp.zeros((pairs, width, columns), F32)
    made = lax.dynamic_update_slice_in_dim(made, jnp.stack([made_0, made_1]), 0, 0)
    residual, made = rounds(residual, made, 2, None)

    flat = made.reshape(pairs * width, columns)
    got = swapped(flat)
    before_whole = in_order(flat[:, :half], got[:, :half], 1)
    here_whole = in_order(flat[:, half:], got[:, half:], 1)
    before_term = ridge_weight * exact_dot(before_whole, before_gram)
    here_term = ridge_weight * exact_dot(here_whole, my_gram)
    carried = exact_dot(before_term, through)
    carried = half_of(carried, core) + swapped(half_of(carried, 1 - core))
    terms = jnp.concatenate([before_term, here_term - carried], 1)
    terms = jnp.where(z == 0, terms, 0.0).reshape(pairs, width, columns)
    residual, more = rounds(residual, jnp.zeros_like(made), 0, terms)

    residual = moved(lax.dynamic_slice_in_dim(residual, core * rows, rows, 1), -1)
    made = made + more
    weights = jnp.stack([moved(made[:, :, :half], -1), made[:, :, half:]], 1)
    order = (position - jnp.arange(blocks)) % blocks
    weights = weights.reshape(blocks, width, half)[order].reshape(blocks * width, half)
    return in_order(weights, swapped(weights), 1), residual


def solution(mesh):
    inner = Mesh(mesh.devices.reshape(-1, HALF, 4, 4), ("z", "core", "x", "y"))
    rows, feat = ("z", "core"), ("x", "y")
    return jax.shard_map(
        local,
        mesh=inner,
        in_specs=(P(rows, feat), P(feat, None), P(feat, rows)),
        out_specs=(P(None, feat), P(feat, rows)),
        check_vma=False,
    )
```
